32 devices in a mesh: loop: 8 (over z, y), row: 4 (over x, core).
Axes of the slice: x: 2, y: 2, z: 4, core: 2. Of those that a mesh axis runs over, the one named last changes fastest.
Arguments:
- slab: float32 [2048, 16384], P('row', 'loop'), may hold values from -6 to 6
- rotations: float32 [32, 512, 512], P('loop', 'row')
- slab_pair: int32 [4], replicated, may hold values from 0 to 31, as said below
Outputs:
- moved: float32 [2048, 16384], P('row', 'loop')
The draws below stay inside these ranges and needn't reach their ends.
Inputs may be any that keep to these rules, and one draw needn't show every extreme that they name: `slab_pair`: distinct pair numbers.
All inputs are finite; a program needn't handle non-finite values.
Results may differ from the reference program's by a relative error of at most 0.00009.
Values sent between devices are 32-bit elements; how exact they have to be, the bound alone decides.
No kernel may reach another device: no remote copies, remote signals or barrier semaphores. Data moves between devices by JAX's collectives and lax.ppermute only.
A program may use at most 64 MiB of HBM per device.

```python
import jax
import jax.numpy as jnp
from jax import lax

B = 256
PAIRS = 32
ORDER = 16384
SLAB_PAIRS = 4
ROWS = 2048


def draw_rotations(key, part):
    width = 2 * B
    noise = jax.random.normal(key, (PAIRS, width, width), jnp.float32)
    eye = jnp.eye(width, dtype=jnp.float32)
    return 0.8 * eye[None] + noise * (0.6 / width ** 0.5)


def draw_slab_pair(key, part):
    inner = jax.random.permutation(jax.random.fold_in(key, 11), PAIRS - 2) + 1
    ends = jnp.array([0, PAIRS - 1], dtype=jnp.int32)
    chosen = jnp.concatenate([ends, inner[:SLAB_PAIRS - 2].astype(jnp.int32)])
    return jax.random.permutation(jax.random.fold_in(key, 23), chosen).astype(jnp.int32)


def steps_of(rng, shape, cuts, low, largest):
    def one(axis_at, parts):
        steps = jax.random.uniform(jax.random.fold_in(jax.random.fold_in(rng, 6), axis_at), (parts,), jnp.float32, low / len(cuts), largest / len(cuts))
        return jnp.repeat(jnp.exp(steps), shape[axis_at] // parts).reshape((-1,) + (1,) * (len(shape) - axis_at - 1))

    factor_of = one(*cuts[0])
    for cut in cuts[1:]:
        factor_of = factor_of * one(*cut)
    return factor_of


def bell_draw(stream_key, shape, scale, bound, cuts=(), kind=jnp.bfloat16):
    result = jax.random.normal(stream_key, shape, jnp.float32) * scale
    if len(cuts) > 0:
        result = steps_of(stream_key, shape, cuts, -0.22, 0.18) * result
    return jnp.clip(result, min=-bound, max=bound).astype(kind)


def setup_inputs(seed: int = 0) -> dict:
    keys = jax.random.split(jax.random.key(seed), 4)
    return {
        "slab": bell_draw(keys[0], (ROWS, ORDER), 1.0, 6.0, ((0, 4), (1, 8)), jnp.float32),
        "rotations": draw_rotations(jax.random.fold_in(keys[3], 71), 0),
        "slab_pair": draw_slab_pair(jax.random.fold_in(keys[3], 71), 0),
    }


def reference(slab, rotations, slab_pair):
    rows_all = slab.shape[0]
    order = slab.shape[1]
    width = 2 * B
    panels = slab.reshape(rows_all, PAIRS, width)
    turned = jnp.einsum("rpi,pij->rpj", panels, rotations, precision=lax.Precision.HIGHEST)
    chosen = jnp.take(rotations, slab_pair.astype(jnp.int32), axis=0)
    grouped = turned.reshape(SLAB_PAIRS, width, order)
    updated = jnp.einsum("tij,tin->tjn", chosen, grouped, precision=lax.Precision.HIGHEST)
    blocks = updated.reshape(rows_all, PAIRS, 2, B)
    tops = blocks[:, :, 0]
    bottoms = blocks[:, :, 1]
    new_tops = jnp.concatenate([tops[:, :1], bottoms[:, :1], tops[:, 1:PAIRS - 1]], axis=1)
    new_bottoms = jnp.concatenate([bottoms[:, 1:], tops[:, PAIRS - 1:]], axis=1)
    return jnp.stack([new_tops, new_bottoms], axis=2).reshape(rows_all, order)
```

```python
from functools import partial

import jax
import jax.numpy as jnp
from jax import lax
from jax.experimental import pallas as pl
from jax.experimental.pallas import tpu as pltpu
from jax.sharding import PartitionSpec as P

VMEM = pl.BlockSpec(memory_space=pltpu.VMEM)
SMEM = pl.BlockSpec(memory_space=pltpu.SMEM)
HBM = pl.BlockSpec(memory_space=pltpu.HBM)
F32, BF16 = jnp.float32, jnp.bfloat16
SPREAD = (0, 2, 1, 3)


def flip(x, axis, bit):
    n = lax.axis_size(axis)
    return lax.ppermute(x, axis, [(i, i ^ bit) for i in range(n)])


def trade(x, first):
    n = lax.axis_size("loop")
    pairs = []
    for i in range(first, n - 1, 2):
        pairs += [(i, i + 1), (i + 1, i)]
    return lax.ppermute(x, "loop", pairs)


def after(x, *others):
    return lax.optimization_barrier((x,) + others)[0]


def params(mib):
    return pltpu.CompilerParams(vmem_limit_bytes=mib << 20)


def cost(flops, bytes_accessed):
    return pl.CostEstimate(flops=flops, bytes_accessed=bytes_accessed, transcendentals=0)


def split(x):
    hi = x.astype(BF16)
    lo = (x - hi.astype(F32)).astype(BF16)
    return hi, lo


def dot3(a_hi, a_lo, b_hi, b_lo):
    def dot(a, b):
        return jnp.dot(a, b, preferred_element_type=F32)

    return dot(a_hi, b_hi) + (dot(a_hi, b_lo) + dot(a_lo, b_hi))


def prepare_kernel(pair_ref, rot_ref, give_ref, keep_ref, edge_ref, rest_ref, sem):
    pairs, piece, width = rot_ref.shape
    half = width // 2
    last = pairs - 1
    side = lax.axis_index("loop") % 2
    away = pl.multiple_of((1 - side) * half, half)
    home = pl.multiple_of(side * half, half)
    copies = []
    for t in range(give_ref.shape[0]):
        copies.append((rot_ref.at[pair_ref[t] % pairs, :, pl.ds(away, half)], give_ref.at[t]))
    copies.append((rot_ref.at[0, :, half:], edge_ref.at[0]))
    copies.append((rot_ref.at[last, :, :half], edge_ref.at[1]))
    for t in range(give_ref.shape[0]):
        copies.append((rot_ref.at[pair_ref[t] % pairs, :, pl.ds(home, half)], keep_ref.at[t]))
    copies.append((rot_ref.at[0, :, :half], rest_ref.at[:, :half]))
    for p in range(1, last):
        copies.append((rot_ref.at[p], rest_ref.at[:, half + (p - 1) * width : half + p * width]))
    copies.append((rot_ref.at[last, :, half:], rest_ref.at[:, half + (last - 1) * width :]))
    copies = [pltpu.make_async_copy(src, dst, sem.at[n]) for n, (src, dst) in enumerate(copies)]
    for copy in copies:
        copy.start()
    for copy in copies:
        copy.wait()


def take(pair_ref, pairs, bit, t, kept, got):
    l = lax.axis_index("loop")
    return jnp.where(((pair_ref[t] // pairs) & bit) == (l & bit), kept, got)


def halve_kernel(pairs, bit, pair_ref, kept_ref, got_ref, give_ref, keep_ref):
    half = give_ref.shape[-1]
    up = (lax.axis_index("loop") // (2 * bit)) % 2
    away = pl.ds(pl.multiple_of((1 - up) * half, half), half)
    home = pl.ds(pl.multiple_of(up * half, half), half)
    for t in range(give_ref.shape[0]):
        give_ref[t] = take(pair_ref, pairs, bit, t, kept_ref[t, :, away], got_ref[t, :, away])
        keep_ref[t] = take(pair_ref, pairs, bit, t, kept_ref[t, :, home], got_ref[t, :, home])


def pick_kernel(pairs, bit, pair_ref, kept_ref, got_ref, out_ref):
    for t in range(out_ref.shape[0]):
        out_ref[t] = take(pair_ref, pairs, bit, t, kept_ref[t], got_ref[t])


def last_pick_kernel(pairs, bit, pair_ref, kept_ref, got_ref, give_ref, keep_ref):
    high = lax.axis_index("row") // 2
    for n in range(2):
        for ref, t in ((give_ref, 2 * (1 - high) + n), (keep_ref, 2 * high + n)):
            ref[n] = take(pair_ref, pairs, bit, t, kept_ref[t], got_ref[t])


def cross_kernel(kept_ref, got_ref, give_ref, keep_ref):
    odd = lax.axis_index("row") % 2
    for n, ref in enumerate((kept_ref, got_ref)):
        give_ref[n] = ref[1 - odd]
        keep_ref[n] = ref[odd]


def join_kernel(a_ref, b_ref, out_ref):
    out_ref[:2] = a_ref[...]
    out_ref[2:] = b_ref[...]


def split_kernel(slab_ref, hi_ref, lo_ref):
    hi_ref[...], lo_ref[...] = split(slab_ref[...])


def stack_parts(hi_ref, lo_ref, n, parts):
    piece, wide = parts[0].shape
    r = lax.axis_index("row")
    for k, part in enumerate(parts):
        rows = pl.ds(pl.multiple_of((r ^ k) * piece, piece), piece)
        hi, lo = split(part)
        hi_ref[n, rows, :wide] = hi
        lo_ref[n, rows, :wide] = lo


def edge_kernel(shi0, slo0, shi1, slo1, own_ref, core0, core1, far_ref, far_core_ref, even_ref, odd_ref, hi_ref, lo_ref):
    side = lax.axis_index("loop") % 2
    for n, core in enumerate((core0, core1)):
        stack_parts(hi_ref, lo_ref, n, (own_ref[n], core[0], far_ref[n], far_core_ref[n]))
    bottom = dot3(shi0[...], slo0[...], hi_ref[0], lo_ref[0])
    top = dot3(shi1[...], slo1[...], hi_ref[1], lo_ref[1])

    @pl.when(side == 0)
    def _():
        even_ref[...] = top
        odd_ref[...] = bottom

    @pl.when(side == 1)
    def _():
        even_ref[...] = bottom
        odd_ref[...] = top


def turn_kernel(
    shi_ref, slo_ref, own_ref, core_ref, far_ref, far_core_ref, even_ref, odd_ref, thi_ref, tlo_ref, hi_ref, lo_ref
):
    pairs, piece, width = core_ref.shape
    half, last = width // 2, pairs - 1
    side = lax.axis_index("loop") % 2
    for p in range(pairs):
        cols = slice(0, half) if p == 0 else slice(half, width) if p == last else slice(0, width)
        at = 0 if p == 0 else half + (p - 1) * width
        here = slice(at, at + cols.stop - cols.start)
        stack_parts(hi_ref, lo_ref, p, (own_ref[:, here], core_ref[p, :, cols], far_ref[:, here], far_core_ref[:, here]))

    def put(block, n):
        hi, lo = split(block)
        thi_ref[n] = hi
        tlo_ref[n] = lo

    for p in range(pairs):
        a_hi, a_lo = (ref[:, p * width : (p + 1) * width] for ref in (shi_ref, slo_ref))
        if p == 0:
            put(dot3(a_hi, a_lo, hi_ref[p, :, :half], lo_ref[p, :, :half]), 0)
        elif p == last:
            put(dot3(a_hi, a_lo, hi_ref[p, :, :half], lo_ref[p, :, :half]), 2 * p + 1)
        else:
            made = dot3(a_hi, a_lo, hi_ref[p], lo_ref[p])
            put(made[:, :half], 2 * p)
            put(made[:, half:], 2 * p + 1)

    @pl.when(side == 0)
    def _():
        put(odd_ref[...], 1)
        put(even_ref[...], 2 * last)

    @pl.when(side == 1)
    def _():
        put(even_ref[...], 1)
        put(odd_ref[...], 2 * last)


def left_kernel(*refs):
    pieces, (thi_ref, tlo_ref, even_ref, odd_ref, out_ref, rot_ref, hi_ref, lo_ref) = refs[:4], refs[4:]
    k = pl.program_id(0)
    blocks = thi_ref.shape[0]
    teams, piece, quarter = pieces[0].shape
    l, loops = lax.axis_index("loop"), lax.axis_size("loop")
    r = lax.axis_index("row")

    @pl.when(k == 0)
    def _():
        mine = 2 * (l % 2) + (l // 2) % 2
        for which, block in enumerate(pieces):
            cols = pl.ds(pl.multiple_of((mine ^ which) * quarter, quarter), quarter)
            for n, there in enumerate(SPREAD):
                rows = pl.ds(pl.multiple_of((r ^ there) * piece, piece), piece)
                rot_ref[rows, cols] = block[n]
        hi_ref[...], lo_ref[...] = split(rot_ref[...].T)

    from_left = (k == 0) & (l > 0)
    from_right = (k == blocks - 1) & (l < loops - 1)
    src = jnp.where(k % 2 == 0, k - 2, k + 2)
    src = jnp.where(l == 0, jnp.where(k == 0, 0, jnp.where(k == 2, 1, src)), src)
    src = jnp.where((l == loops - 1) & (k == blocks - 1), blocks - 2, src)

    @pl.when(jnp.logical_not(from_left | from_right))
    def _():
        out_ref[...] = dot3(hi_ref[...], lo_ref[...], thi_ref[src], tlo_ref[src])

    by_even = (from_left & (l % 2 == 1)) | (from_right & (l % 2 == 0))
    by_odd = (from_left & (l % 2 == 0)) | (from_right & (l % 2 == 1))

    @pl.when(by_even)
    def _():
        out_ref[...] = dot3(hi_ref[...], lo_ref[...], *split(even_ref[...]))

    @pl.when(by_odd)
    def _():
        out_ref[...] = dot3(hi_ref[...], lo_ref[...], *split(odd_ref[...]))


def per_device(slab, rotations, slab_pair):
    pairs, piece, width = rotations.shape
    half, quarter = width // 2, width // 4
    rows, columns = slab.shape
    loops, teams = lax.axis_size("loop"), lax.axis_size("row")
    last = pairs - 1
    array = jax.ShapeDtypeStruct

    def glue(kernel, shapes, *operands, pair=False):
        return pl.pallas_call(
            kernel,
            out_shape=tuple(array(shape, F32) for shape in shapes),
            in_specs=[SMEM] * pair + [VMEM] * len(operands),
            out_specs=(VMEM,) * len(shapes),
            compiler_params=params(4),
            cost_estimate=cost(0, 0),
        )(*([slab_pair] * pair), *operands)

    give, keep, edge, rest = pl.pallas_call(
        prepare_kernel,
        out_shape=(
            array((teams, piece, half), F32),
            array((teams, piece, half), F32),
            array((2, piece, half), F32),
            array((piece, last * width), F32),
        ),
        in_specs=[SMEM, HBM],
        out_specs=(VMEM,) * 4,
        scratch_shapes=[pltpu.SemaphoreType.DMA((2 * teams + 2 + pairs,))],
        compiler_params=params(8),
        cost_estimate=cost(0, 0),
    )(slab_pair, pltpu.with_memory_space_constraint(rotations, pltpu.HBM))

    got = flip(give, "loop", 1)
    far_edge = flip(edge, "row", 2)
    core = flip(rotations, "row", 1)

    slab_hi, slab_lo = pl.pallas_call(
        split_kernel,
        grid=(4,),
        out_shape=(array((rows, columns), BF16),) * 2,
        in_specs=[pl.BlockSpec((rows // 4, columns), lambda i: (i, 0))],
        out_specs=(pl.BlockSpec((rows // 4, columns), lambda i: (i, 0)),) * 2,
        compiler_params=params(8),
        cost_estimate=cost(0, 0),
    )(pltpu.with_memory_space_constraint(after(slab, give), pltpu.HBM))

    far_edge = after(far_edge, slab_hi)
    far_core_edge = flip(far_edge, "row", 1)
    far = flip(after(rest, far_edge), "row", 2)

    even, odd = pl.pallas_call(
        edge_kernel,
        grid=(1,),
        out_shape=(array((rows, half), F32),) * 2,
        in_specs=[
            pl.BlockSpec((rows, width), lambda i: (0, 0)),
            pl.BlockSpec((rows, width), lambda i: (0, 0)),
            pl.BlockSpec((rows, width), lambda i: (0, last)),
            pl.BlockSpec((rows, width), lambda i: (0, last)),
            pl.BlockSpec((2, piece, half), lambda i: (0, 0, 0)),
            pl.BlockSpec((1, piece, half), lambda i: (0, 0, 1)),
            pl.BlockSpec((1, piece, half), lambda i: (last, 0, 0)),
            pl.BlockSpec((2, piece, half), lambda i: (0, 0, 0)),
            pl.BlockSpec((2, piece, half), lambda i: (0, 0, 0)),
        ],
        out_specs=(pl.BlockSpec((rows, half), lambda i: (0, 0)),) * 2,
        scratch_shapes=[pltpu.VMEM((2, width, half), BF16)] * 2,
        compiler_params=params(20),
        cost_estimate=cost(0, 0),
    )(slab_hi, slab_lo, slab_hi, slab_lo, edge, core, core, far_edge, far_core_edge)
    even_in = trade(even, 0)
    odd_in = trade(odd, 1)

    quarters = (teams, piece, quarter)
    give, held = glue(partial(halve_kernel, pairs, 1), (quarters, quarters), keep, after(got, even), pair=True)
    got = flip(give, "loop", 2)
    far = after(far, got)
    far_core = flip(far, "row", 1)
    blocks = array((2 * pairs, rows, half), BF16)
    turned_hi, turned_lo = pl.pallas_call(
        turn_kernel,
        out_shape=(blocks, blocks),
        in_specs=[VMEM] * 8,
        out_specs=(VMEM, VMEM),
        scratch_shapes=[pltpu.VMEM((pairs, width, width), BF16)] * 2,
        compiler_params=params(28),
        cost_estimate=cost(0, 0),
    )(slab_hi, slab_lo, rest, core, far, far_core, even, odd)

    bits = [1 << b for b in range(1, (loops - 1).bit_length())]
    for bit in bits[:-1]:
        (held,) = glue(partial(pick_kernel, pairs, bit), (quarters,), held, got, pair=True)
        got = flip(held, "loop", 2 * bit)
    got = after(got, turned_hi, even_in, odd_in)
    pieces = (2, piece, quarter)
    give, held = glue(partial(last_pick_kernel, pairs, bits[-1]), (pieces, pieces), held, got, pair=True)
    give, held = glue(cross_kernel, (pieces, pieces), held, flip(give, "row", 2))
    (held,) = glue(join_kernel, (quarters,), held, flip(give, "row", 1))

    near = flip(held, "loop", 2)
    side = flip(held, "loop", 1)
    across = flip(side, "loop", 2)

    return pl.pallas_call(
        left_kernel,
        grid=(2 * pairs,),
        out_shape=array((rows, columns), F32),
        in_specs=[VMEM] * 8,
        out_specs=pl.BlockSpec((rows, half), lambda k: (0, k)),
        scratch_shapes=[pltpu.VMEM((width, width), F32)] + [pltpu.VMEM((width, width), BF16)] * 2,
        compiler_params=params(28),
        cost_estimate=cost(0, 0),
    )(held, near, side, across, turned_hi, turned_lo, even_in, odd_in)


def solution(mesh):
    return jax.shard_map(
        per_device,
        mesh=mesh,
        in_specs=(P("row", "loop"), P("loop", "row", None), P()),
        out_specs=P("row", "loop"),
        check_vma=False,
    )
```

```python
from functools import partial

import jax
import jax.numpy as jnp
from jax import lax
from jax.experimental import pallas as pl
from jax.experimental.pallas import tpu as pltpu
from jax.sharding import PartitionSpec as P

VMEM = pl.BlockSpec(memory_space=pltpu.VMEM)
SMEM = pl.BlockSpec(memory_space=pltpu.SMEM)
HBM = pl.BlockSpec(memory_space=pltpu.HBM)
F32, BF16 = jnp.float32, jnp.bfloat16


def flip(x, axis, bit):
    n = lax.axis_size(axis)
    return lax.ppermute(x, axis, [(i, i ^ bit) for i in range(n)])


def trade(x, first):
    n = lax.axis_size("loop")
    pairs = []
    for i in range(first, n - 1, 2):
        pairs += [(i, i + 1), (i + 1, i)]
    return lax.ppermute(x, "loop", pairs)


def after(x, *others):
    return lax.optimization_barrier((x,) + others)[0]


def params(mib):
    return pltpu.CompilerParams(vmem_limit_bytes=mib << 20)


def cost(flops, bytes_accessed):
    return pl.CostEstimate(flops=flops, bytes_accessed=bytes_accessed, transcendentals=0)


def split(x):
    hi = x.astype(BF16)
    lo = (x - hi.astype(F32)).astype(BF16)
    return hi, lo


def dot3(a_hi, a_lo, b_hi, b_lo):
    def dot(a, b):
        return jnp.dot(a, b, preferred_element_type=F32)

    return dot(a_hi, b_hi) + (dot(a_hi, b_lo) + dot(a_lo, b_hi))


def copy_all(copies, sem):
    copies = [pltpu.make_async_copy(src, dst, sem.at[n]) for n, (src, dst) in enumerate(copies)]
    for copy in copies:
        copy.start()
    for copy in copies:
        copy.wait()


def candidate_kernel(home, pair_ref, rot_ref, a_ref, b_ref, sem):
    pairs, piece, width = rot_ref.shape
    chunk, half, quarter = piece // 2, width // 2, width // 4
    l = lax.axis_index("loop")
    side, up = l % 2, (l // 2) % 2
    if not home:
        side, up = 1 - side, 1 - up
    copies = []
    for t in range(a_ref.shape[0]):
        slot = pair_ref[t] % pairs
        copies.append((rot_ref.at[slot, :chunk, pl.ds(pl.multiple_of(side * half, half), half)], a_ref.at[t]))
        for s in range(2):
            cols = pl.ds(pl.multiple_of(s * half + up * quarter, quarter), quarter)
            copies.append((rot_ref.at[slot, chunk:, cols], b_ref.at[t, :, s * quarter : (s + 1) * quarter]))
    copy_all(copies, sem)


def cut_kernel(rot_ref, edge_ref, rest_ref, sem):
    pairs, _, width = rot_ref.shape
    half, last = width // 2, pairs - 1
    copies = [
        (rot_ref.at[0, :, half:], edge_ref.at[0]),
        (rot_ref.at[last, :, :half], edge_ref.at[1]),
        (rot_ref.at[0, :, :half], rest_ref.at[:, :half]),
        (rot_ref.at[last, :, half:], rest_ref.at[:, half + (last - 1) * width :]),
    ]
    for p in range(1, last):
        copies.append((rot_ref.at[p], rest_ref.at[:, half + (p - 1) * width : half + p * width]))
    copy_all(copies, sem)


def take(pair_ref, pairs, bit, t, kept, got):
    l = lax.axis_index("loop")
    return jnp.where(((pair_ref[t] // pairs) & bit) == (l & bit), kept, got)


def halve_kernel(pairs, pair_ref, a_kept, b_kept, a_got, b_got, a_give, b_give, a_keep, b_keep):
    l = lax.axis_index("loop")
    quarter = a_give.shape[-1]
    side, up = l % 2, (l // 2) % 2
    for bit, cut, kept, got, give, keep in (
        (1, up, a_kept, a_got, a_give, a_keep),
        (2, side, b_kept, b_got, b_give, b_keep),
    ):
        away = pl.ds(pl.multiple_of((1 - cut) * quarter, quarter), quarter)
        home = pl.ds(pl.multiple_of(cut * quarter, quarter), quarter)
        for t in range(give.shape[0]):
            give[t] = take(pair_ref, pairs, bit, t, kept[t, :, away], got[t, :, away])
            keep[t] = take(pair_ref, pairs, bit, t, kept[t, :, home], got[t, :, home])


def meet_kernel(pairs, pair_ref, a_kept, b_kept, a_got, b_got, out_ref):
    chunk = a_kept.shape[1]
    for t in range(out_ref.shape[0]):
        out_ref[t, :chunk] = take(pair_ref, pairs, 2, t, a_kept[t], a_got[t])
        out_ref[t, chunk:] = take(pair_ref, pairs, 1, t, b_kept[t], b_got[t])


def pick_kernel(pairs, bit, pair_ref, kept_ref, got_ref, out_ref):
    for t in range(out_ref.shape[0]):
        out_ref[t] = take(pair_ref, pairs, bit, t, kept_ref[t], got_ref[t])


def last_pick_kernel(pairs, bit, pair_ref, kept_ref, got_ref, give_ref, keep_ref):
    high = lax.axis_index("row") // 2
    for n in range(2):
        for ref, t in ((give_ref, 2 * (1 - high) + n), (keep_ref, 2 * high + n)):
            ref[n] = take(pair_ref, pairs, bit, t, kept_ref[t], got_ref[t])


def cross_kernel(kept_ref, got_ref, give_ref, keep_ref):
    odd = lax.axis_index("row") % 2
    for n, ref in enumerate((kept_ref, got_ref)):
        give_ref[n] = ref[1 - odd]
        keep_ref[n] = ref[odd]


def split_kernel(slab_ref, hi_ref, lo_ref):
    hi_ref[...], lo_ref[...] = split(slab_ref[...])


def stack_parts(hi_ref, lo_ref, n, parts):
    piece, wide = parts[0].shape
    r = lax.axis_index("row")
    for k, part in enumerate(parts):
        rows = pl.ds(pl.multiple_of((r ^ k) * piece, piece), piece)
        hi, lo = split(part)
        hi_ref[n, rows, :wide] = hi
        lo_ref[n, rows, :wide] = lo


def edge_kernel(shi0, slo0, shi1, slo1, own_ref, core0, core1, far_ref, far_core_ref, even_ref, odd_ref, hi_ref, lo_ref):
    side = lax.axis_index("loop") % 2
    for n, core in enumerate((core0, core1)):
        stack_parts(hi_ref, lo_ref, n, (own_ref[n], core[0], far_ref[n], far_core_ref[n]))
    bottom = dot3(shi0[...], slo0[...], hi_ref[0], lo_ref[0])
    top = dot3(shi1[...], slo1[...], hi_ref[1], lo_ref[1])

    @pl.when(side == 0)
    def _():
        even_ref[...] = top
        odd_ref[...] = bottom

    @pl.when(side == 1)
    def _():
        even_ref[...] = bottom
        odd_ref[...] = top


def turn_kernel(
    shi_ref, slo_ref, own_ref, core_ref, far_ref, far_core_ref, even_ref, odd_ref, thi_ref, tlo_ref, hi_ref, lo_ref
):
    pairs, piece, width = core_ref.shape
    half, last = width // 2, pairs - 1
    side = lax.axis_index("loop") % 2
    for p in range(pairs):
        cols = slice(0, half) if p == 0 else slice(half, width) if p == last else slice(0, width)
        at = 0 if p == 0 else half + (p - 1) * width
        here = slice(at, at + cols.stop - cols.start)
        stack_parts(hi_ref, lo_ref, p, (own_ref[:, here], core_ref[p, :, cols], far_ref[:, here], far_core_ref[:, here]))

    def put(block, n):
        hi, lo = split(block)
        thi_ref[n] = hi
        tlo_ref[n] = lo

    for p in range(pairs):
        a_hi, a_lo = (ref[:, p * width : (p + 1) * width] for ref in (shi_ref, slo_ref))
        if p == 0:
            put(dot3(a_hi, a_lo, hi_ref[p, :, :half], lo_ref[p, :, :half]), 0)
        elif p == last:
            put(dot3(a_hi, a_lo, hi_ref[p, :, :half], lo_ref[p, :, :half]), 2 * p + 1)
        else:
            made = dot3(a_hi, a_lo, hi_ref[p], lo_ref[p])
            put(made[:, :half], 2 * p)
            put(made[:, half:], 2 * p + 1)

    @pl.when(side == 0)
    def _():
        put(odd_ref[...], 1)
        put(even_ref[...], 2 * last)

    @pl.when(side == 1)
    def _():
        put(even_ref[...], 1)
        put(odd_ref[...], 2 * last)


def left_kernel(*refs):
    pieces, (thi_ref, tlo_ref, even_ref, odd_ref, out_ref, rot_ref, hi_ref, lo_ref) = refs[:8], refs[8:]
    k = pl.program_id(0)
    blocks = thi_ref.shape[0]
    _, piece, quarter = pieces[0].shape
    l, loops = lax.axis_index("loop"), lax.axis_size("loop")
    r = lax.axis_index("row")

    @pl.when(k == 0)
    def _():
        mine = 2 * (l % 2) + (l // 2) % 2
        for place, block in enumerate(pieces):
            which, core = divmod(place, 2)
            cols = pl.ds(pl.multiple_of((mine ^ which) * quarter, quarter), quarter)
            for n in range(2):
                rows = pl.ds(pl.multiple_of((r ^ (2 * n + core)) * piece, piece), piece)
                rot_ref[rows, cols] = block[n]
        hi_ref[...], lo_ref[...] = split(rot_ref[...].T)

    from_left = (k == 0) & (l > 0)
    from_right = (k == blocks - 1) & (l < loops - 1)
    src = jnp.where(k % 2 == 0, k - 2, k + 2)
    src = jnp.where(l == 0, jnp.where(k == 0, 0, jnp.where(k == 2, 1, src)), src)
    src = jnp.where((l == loops - 1) & (k == blocks - 1), blocks - 2, src)

    @pl.when(jnp.logical_not(from_left | from_right))
    def _():
        out_ref[...] = dot3(hi_ref[...], lo_ref[...], thi_ref[src], tlo_ref[src])

    by_even = (from_left & (l % 2 == 1)) | (from_right & (l % 2 == 0))
    by_odd = (from_left & (l % 2 == 0)) | (from_right & (l % 2 == 1))

    @pl.when(by_even)
    def _():
        out_ref[...] = dot3(hi_ref[...], lo_ref[...], *split(even_ref[...]))

    @pl.when(by_odd)
    def _():
        out_ref[...] = dot3(hi_ref[...], lo_ref[...], *split(odd_ref[...]))


def per_device(slab, rotations, slab_pair):
    pairs, piece, width = rotations.shape
    half, quarter = width // 2, width // 4
    rows, columns = slab.shape
    loops, teams = lax.axis_size("loop"), lax.axis_size("row")
    last = pairs - 1
    array = jax.ShapeDtypeStruct

    def glue(kernel, shapes, *operands, pair=False):
        return pl.pallas_call(
            kernel,
            out_shape=tuple(array(shape, F32) for shape in shapes),
            in_specs=[SMEM] * pair + [VMEM] * len(operands),
            out_specs=(VMEM,) * len(shapes),
            compiler_params=params(4),
            cost_estimate=cost(0, 0),
        )(*([slab_pair] * pair), *operands)

    def copied(kernel, shapes, count, pair=False):
        return pl.pallas_call(
            kernel,
            out_shape=tuple(array(shape, F32) for shape in shapes),
            in_specs=[SMEM] * pair + [HBM],
            out_specs=(VMEM,) * len(shapes),
            scratch_shapes=[pltpu.SemaphoreType.DMA((count,))],
            compiler_params=params(4),
            cost_estimate=cost(0, 0),
        )

    transforms = pltpu.with_memory_space_constraint(rotations, pltpu.HBM)
    chunks = (teams, piece // 2, half)
    a_give, b_give = copied(partial(candidate_kernel, False), (chunks, chunks), 3 * teams, pair=True)(
        slab_pair, transforms
    )
    edge, rest = copied(cut_kernel, ((2, piece, half), (piece, last * width)), pairs + 2)(
        after(transforms, a_give)
    )
    a_keep, b_keep = copied(partial(candidate_kernel, True), (chunks, chunks), 3 * teams, pair=True)(
        slab_pair, after(transforms, edge)
    )

    a_got = flip(a_give, "loop", 1)
    b_got = flip(b_give, "loop", 2)
    far_edge = flip(edge, "row", 2)
    core = flip(rotations, "row", 1)

    slab_hi, slab_lo = pl.pallas_call(
        split_kernel,
        grid=(4,),
        out_shape=(array((rows, columns), BF16),) * 2,
        in_specs=[pl.BlockSpec((rows // 4, columns), lambda i: (i, 0))],
        out_specs=(pl.BlockSpec((rows // 4, columns), lambda i: (i, 0)),) * 2,
        compiler_params=params(8),
        cost_estimate=cost(0, 0),
    )(pltpu.with_memory_space_constraint(after(slab, a_keep), pltpu.HBM))

    fine = (teams, piece // 2, quarter)
    a_give, b_give, a_keep, b_keep = glue(
        partial(halve_kernel, pairs), (fine,) * 4, a_keep, b_keep, a_got, b_got, pair=True
    )
    a_got = flip(a_give, "loop", 2)
    b_got = flip(b_give, "loop", 1)
    far_edge = after(far_edge, slab_hi, a_got, b_got)
    quarters = (teams, piece, quarter)
    (held,) = glue(partial(meet_kernel, pairs), (quarters,), a_keep, b_keep, a_got, b_got, pair=True)
    far_core_edge = after(flip(far_edge, "row", 1), held)
    far = flip(after(rest, far_edge), "row", 2)

    even, odd = pl.pallas_call(
        edge_kernel,
        grid=(1,),
        out_shape=(array((rows, half), F32),) * 2,
        in_specs=[
            pl.BlockSpec((rows, width), lambda i: (0, 0)),
            pl.BlockSpec((rows, width), lambda i: (0, 0)),
            pl.BlockSpec((rows, width), lambda i: (0, last)),
            pl.BlockSpec((rows, width), lambda i: (0, last)),
            pl.BlockSpec((2, piece, half), lambda i: (0, 0, 0)),
            pl.BlockSpec((1, piece, half), lambda i: (0, 0, 1)),
            pl.BlockSpec((1, piece, half), lambda i: (last, 0, 0)),
            pl.BlockSpec((2, piece, half), lambda i: (0, 0, 0)),
            pl.BlockSpec((2, piece, half), lambda i: (0, 0, 0)),
        ],
        out_specs=(pl.BlockSpec((rows, half), lambda i: (0, 0)),) * 2,
        scratch_shapes=[pltpu.VMEM((2, width, half), BF16)] * 2,
        compiler_params=params(20),
        cost_estimate=cost(0, 0),
    )(slab_hi, slab_lo, slab_hi, slab_lo, edge, core, core, far_edge, far_core_edge)
    even_in = trade(even, 0)
    odd_in = trade(after(odd, even_in), 1)

    bits = [1 << b for b in range(2, (loops - 1).bit_length())]
    got = flip(held, "loop", bits[0])
    for bit in bits[:-1]:
        (held,) = glue(partial(pick_kernel, pairs, bit), (quarters,), held, got, pair=True)
        got = flip(held, "loop", 2 * bit)
    far_core = flip(after(far, even_in, got), "row", 1)
    blocks = array((2 * pairs, rows, half), BF16)
    turned_hi, turned_lo = pl.pallas_call(
        turn_kernel,
        out_shape=(blocks, blocks),
        in_specs=[VMEM] * 8,
        out_specs=(VMEM, VMEM),
        scratch_shapes=[pltpu.VMEM((pairs, width, width), BF16)] * 2,
        compiler_params=params(28),
        cost_estimate=cost(0, 0),
    )(slab_hi, slab_lo, rest, core, far, far_core, even, odd)

    pieces = (2, piece, quarter)
    give, held = glue(partial(last_pick_kernel, pairs, bits[-1]), (pieces, pieces), held, got, pair=True)
    give, held = glue(cross_kernel, (pieces, pieces), held, after(flip(give, "row", 2), odd_in))
    more = flip(give, "row", 1)

    near = flip(held, "loop", 2), flip(more, "loop", 2)
    side = flip(held, "loop", 1), flip(more, "loop", 1)
    across = flip(near[0], "loop", 1), flip(side[1], "loop", 2)

    return pl.pallas_call(
        left_kernel,
        grid=(2 * pairs,),
        out_shape=array((rows, columns), F32),
        in_specs=[VMEM] * 12,
        out_specs=pl.BlockSpec((rows, half), lambda k: (0, k)),
        scratch_shapes=[pltpu.VMEM((width, width), F32)] + [pltpu.VMEM((width, width), BF16)] * 2,
        compiler_params=params(28),
        cost_estimate=cost(0, 0),
    )(held, more, *near, *side, *across, turned_hi, turned_lo, even_in, odd_in)


def solution(mesh):
    return jax.shard_map(
        per_device,
        mesh=mesh,
        in_specs=(P("row", "loop"), P("loop", "row", None), P()),
        out_specs=P("row", "loop"),
        check_vma=False,
    )
```

```python
from functools import partial

import jax
import jax.numpy as jnp
from jax import lax
from jax.experimental import pallas as pl
from jax.experimental.pallas import tpu as pltpu
from jax.sharding import PartitionSpec as P

VMEM = pl.BlockSpec(memory_space=pltpu.VMEM)
SMEM = pl.BlockSpec(memory_space=pltpu.SMEM)
HBM = pl.BlockSpec(memory_space=pltpu.HBM)
F32, BF16 = jnp.float32, jnp.bfloat16


def flip(x, axis, bit):
    n = lax.axis_size(axis)
    return lax.ppermute(x, axis, [(i, i ^ bit) for i in range(n)])


def trade(x, first):
    n = lax.axis_size("loop")
    pairs = []
    for i in range(first, n - 1, 2):
        pairs += [(i, i + 1), (i + 1, i)]
    return lax.ppermute(x, "loop", pairs)


def after(x, *others):
    return lax.optimization_barrier((x,) + others)[0]


def params(mib):
    return pltpu.CompilerParams(vmem_limit_bytes=mib << 20)


def cost(flops, bytes_accessed):
    return pl.CostEstimate(flops=flops, bytes_accessed=bytes_accessed, transcendentals=0)


def split(x):
    hi = x.astype(BF16)
    lo = (x - hi.astype(F32)).astype(BF16)
    return hi, lo


def dot3(a_hi, a_lo, b_hi, b_lo):
    def dot(a, b):
        return jnp.dot(a, b, preferred_element_type=F32)

    return dot(a_hi, b_hi) + (dot(a_hi, b_lo) + dot(a_lo, b_hi))


def copy_all(copies, sem):
    copies = [pltpu.make_async_copy(src, dst, sem.at[n]) for n, (src, dst) in enumerate(copies)]
    for copy in copies:
        copy.start()
    for copy in copies:
        copy.wait()


def candidate_kernel(home, pair_ref, rot_ref, a_ref, b_ref, sem):
    pairs, piece, width = rot_ref.shape
    chunk, half, quarter = piece // 2, width // 2, width // 4
    l = lax.axis_index("loop")
    side, up = l % 2, (l // 2) % 2
    if not home:
        side, up = 1 - side, 1 - up
    copies = []
    for t in range(a_ref.shape[0]):
        slot = pair_ref[t] % pairs
        copies.append((rot_ref.at[slot, :chunk, pl.ds(pl.multiple_of(side * half, half), half)], a_ref.at[t]))
        for s in range(2):
            cols = pl.ds(pl.multiple_of(s * half + up * quarter, quarter), quarter)
            copies.append((rot_ref.at[slot, chunk:, cols], b_ref.at[t, :, s * quarter : (s + 1) * quarter]))
    copy_all(copies, sem)


def cut_kernel(rot_ref, edge_ref, rest_ref, sem):
    pairs, _, width = rot_ref.shape
    half, last = width // 2, pairs - 1
    copies = [
        (rot_ref.at[0, :, half:], edge_ref.at[0]),
        (rot_ref.at[last, :, :half], edge_ref.at[1]),
        (rot_ref.at[0, :, :half], rest_ref.at[:, :half]),
        (rot_ref.at[last, :, half:], rest_ref.at[:, half + (last - 1) * width :]),
    ]
    for p in range(1, last):
        copies.append((rot_ref.at[p], rest_ref.at[:, half + (p - 1) * width : half + p * width]))
    copy_all(copies, sem)


def take(pair_ref, pairs, bit, t, kept, got):
    l = lax.axis_index("loop")
    return jnp.where(((pair_ref[t] // pairs) & bit) == (l & bit), kept, got)


def halve_kernel(pairs, pair_ref, a_kept, b_kept, a_got, b_got, a_give, b_give, a_keep, b_keep):
    l = lax.axis_index("loop")
    quarter = a_give.shape[-1]
    side, up = l % 2, (l // 2) % 2
    for bit, cut, kept, got, give, keep in (
        (1, up, a_kept, a_got, a_give, a_keep),
        (2, side, b_kept, b_got, b_give, b_keep),
    ):
        away = pl.ds(pl.multiple_of((1 - cut) * quarter, quarter), quarter)
        home = pl.ds(pl.multiple_of(cut * quarter, quarter), quarter)
        for t in range(give.shape[0]):
            give[t] = take(pair_ref, pairs, bit, t, kept[t, :, away], got[t, :, away])
            keep[t] = take(pair_ref, pairs, bit, t, kept[t, :, home], got[t, :, home])


def meet_kernel(pairs, pair_ref, a_kept, b_kept, a_got, b_got, out_ref):
    chunk = a_kept.shape[1]
    for t in range(out_ref.shape[0]):
        out_ref[t, :chunk] = take(pair_ref, pairs, 2, t, a_kept[t], a_got[t])
        out_ref[t, chunk:] = take(pair_ref, pairs, 1, t, b_kept[t], b_got[t])


def pick_kernel(pairs, bit, pair_ref, kept_ref, got_ref, out_ref):
    for t in range(out_ref.shape[0]):
        out_ref[t] = take(pair_ref, pairs, bit, t, kept_ref[t], got_ref[t])


def last_pick_kernel(pairs, bit, pair_ref, kept_ref, got_ref, give_ref, keep_ref):
    high = lax.axis_index("row") // 2
    for n in range(2):
        for ref, t in ((give_ref, 2 * (1 - high) + n), (keep_ref, 2 * high + n)):
            ref[n] = take(pair_ref, pairs, bit, t, kept_ref[t], got_ref[t])


def cross_kernel(kept_ref, got_ref, give_ref, keep_ref):
    odd = lax.axis_index("row") % 2
    for n, ref in enumerate((kept_ref, got_ref)):
        give_ref[n] = ref[1 - odd]
        keep_ref[n] = ref[odd]


def split_kernel(slab_ref, hi_ref, lo_ref):
    hi_ref[...], lo_ref[...] = split(slab_ref[...])


def stack_parts(hi_ref, lo_ref, n, parts):
    piece, wide = parts[0].shape
    r = lax.axis_index("row")
    for k, part in enumerate(parts):
        rows = pl.ds(pl.multiple_of((r ^ k) * piece, piece), piece)
        hi, lo = split(part)
        hi_ref[n, rows, :wide] = hi
        lo_ref[n, rows, :wide] = lo


def edge_kernel(shi0, slo0, shi1, slo1, own_ref, core0, core1, far_ref, far_core_ref, even_ref, odd_ref, hi_ref, lo_ref):
    side = lax.axis_index("loop") % 2
    for n, core in enumerate((core0, core1)):
        stack_parts(hi_ref, lo_ref, n, (own_ref[n], core[0], far_ref[n], far_core_ref[n]))
    bottom = dot3(shi0[...], slo0[...], hi_ref[0], lo_ref[0])
    top = dot3(shi1[...], slo1[...], hi_ref[1], lo_ref[1])

    @pl.when(side == 0)
    def _():
        even_ref[...] = top
        odd_ref[...] = bottom

    @pl.when(side == 1)
    def _():
        even_ref[...] = bottom
        odd_ref[...] = top


def turn_kernel(
    shi_ref, slo_ref, own_ref, core_ref, far_ref, far_core_ref, even_ref, odd_ref, even_in,
    thi_ref, tlo_ref, hi_ref, lo_ref,
):
    pairs, piece, width = core_ref.shape
    half, last = width // 2, pairs - 1
    l, loops = lax.axis_index("loop"), lax.axis_size("loop")
    for p in range(pairs):
        cols = slice(0, half) if p == 0 else slice(half, width) if p == last else slice(0, width)
        at = 0 if p == 0 else half + (p - 1) * width
        here = slice(at, at + cols.stop - cols.start)
        stack_parts(hi_ref, lo_ref, p, (own_ref[:, here], core_ref[p, :, cols], far_ref[:, here], far_core_ref[:, here]))

    def put(block, k):
        hi, lo = split(block)
        thi_ref[:, k * half : (k + 1) * half] = hi
        tlo_ref[:, k * half : (k + 1) * half] = lo

    for p in range(1, last):
        a_hi, a_lo = (ref[:, p * width : (p + 1) * width] for ref in (shi_ref, slo_ref))
        made = dot3(a_hi, a_lo, hi_ref[p], lo_ref[p])
        put(made[:, :half], 2 * (p + 1))
        put(made[:, half:], 2 * (p - 1) + 1)
    a_hi, a_lo = (ref[:, last * width :] for ref in (shi_ref, slo_ref))
    put(dot3(a_hi, a_lo, hi_ref[last, :, :half], lo_ref[last, :, :half]), 2 * (last - 1) + 1)
    a_hi, a_lo = (ref[:, :width] for ref in (shi_ref, slo_ref))
    top = dot3(a_hi, a_lo, hi_ref[0, :, :half], lo_ref[0, :, :half])
    put(jnp.where(l == 0, top, even_in[...]), 0)
    put(jnp.where(l == 0, odd_ref[...], top), 2)
    put(jnp.where(l == loops - 1, odd_ref[...], even_in[...]), 2 * pairs - 1)


def left_kernel(offsets, aliased, *refs):
    count = 2 * len(offsets)
    pieces, (thi_ref, tlo_ref, odd_ref) = refs[:count], refs[count : count + 3]
    out_ref, made_ref, rot_ref, hi_ref, lo_ref, sem = refs[count + 3 + aliased :]
    _, piece, quarter = pieces[0].shape
    width = thi_ref.shape[0]
    l, r = lax.axis_index("loop"), lax.axis_index("row")
    mine = 2 * (l % 2) + (l // 2) % 2
    for place, block in enumerate(pieces):
        n, core = divmod(place, 2)
        for m in range(2):
            rows = pl.ds(pl.multiple_of((r ^ (2 * m + core)) * piece, piece), piece)
            rot_ref[rows, n * quarter : (n + 1) * quarter] = block[m]
    hi_ref[...], lo_ref[...] = split(rot_ref[...].T)
    wide = width // 2
    blocks = made_ref.shape[1] // wide
    loops = lax.axis_size("loop")
    by_odd = {0: (l % 2 == 0) & (l > 0), blocks - 1: (l % 2 == 1) & (l < loops - 1)}
    copies = []
    for k in (*range(1, blocks - 1), 0, blocks - 1):
        cols = slice(k * wide, (k + 1) * wide)
        t_hi, t_lo = thi_ref[:, cols], tlo_ref[:, cols]
        if k in by_odd:
            came_hi, came_lo = split(odd_ref[...])
            t_hi, t_lo = jnp.where(by_odd[k], came_hi, t_hi), jnp.where(by_odd[k], came_lo, t_lo)
        made_ref[:, cols] = dot3(hi_ref[...], lo_ref[...], t_hi, t_lo)
        for n, offset in enumerate(offsets):
            rows = pl.ds(pl.multiple_of((mine ^ offset) * quarter, quarter), quarter)
            copy = pltpu.make_async_copy(
                made_ref.at[n * quarter : (n + 1) * quarter, cols], out_ref.at[rows, cols], sem.at[n, k]
            )
            copy.start()
            copies.append(copy)
    for copy in copies:
        copy.wait()


def per_device(slab, rotations, slab_pair):
    pairs, piece, width = rotations.shape
    half, quarter = width // 2, width // 4
    rows, columns = slab.shape
    loops, teams = lax.axis_size("loop"), lax.axis_size("row")
    last = pairs - 1
    array = jax.ShapeDtypeStruct

    def glue(kernel, shapes, *operands, pair=False):
        return pl.pallas_call(
            kernel,
            out_shape=tuple(array(shape, F32) for shape in shapes),
            in_specs=[SMEM] * pair + [VMEM] * len(operands),
            out_specs=(VMEM,) * len(shapes),
            compiler_params=params(4),
            cost_estimate=cost(0, 0),
        )(*([slab_pair] * pair), *operands)

    def copied(kernel, shapes, count, pair=False):
        return pl.pallas_call(
            kernel,
            out_shape=tuple(array(shape, F32) for shape in shapes),
            in_specs=[SMEM] * pair + [HBM],
            out_specs=(VMEM,) * len(shapes),
            scratch_shapes=[pltpu.SemaphoreType.DMA((count,))],
            compiler_params=params(4),
            cost_estimate=cost(0, 0),
        )

    transforms = pltpu.with_memory_space_constraint(rotations, pltpu.HBM)
    chunks = (teams, piece // 2, half)
    a_give, b_give = copied(partial(candidate_kernel, False), (chunks, chunks), 3 * teams, pair=True)(
        slab_pair, transforms
    )
    edge, rest = copied(cut_kernel, ((2, piece, half), (piece, last * width)), pairs + 2)(after(transforms, a_give))
    a_keep, b_keep = copied(partial(candidate_kernel, True), (chunks, chunks), 3 * teams, pair=True)(
        slab_pair, after(transforms, edge)
    )

    a_got = flip(a_give, "loop", 1)
    b_got = flip(b_give, "loop", 2)
    far_edge = flip(edge, "row", 2)
    core = flip(rotations, "row", 1)

    slab_hi, slab_lo = pl.pallas_call(
        split_kernel,
        grid=(4,),
        out_shape=(array((rows, columns), BF16),) * 2,
        in_specs=[pl.BlockSpec((rows // 4, columns), lambda i: (i, 0))],
        out_specs=(pl.BlockSpec((rows // 4, columns), lambda i: (i, 0)),) * 2,
        compiler_params=params(8),
        cost_estimate=cost(0, 0),
    )(pltpu.with_memory_space_constraint(after(slab, a_keep), pltpu.HBM))

    fine = (teams, piece // 2, quarter)
    a_give, b_give, a_keep, b_keep = glue(
        partial(halve_kernel, pairs), (fine,) * 4, a_keep, b_keep, after(a_got, slab_hi), b_got, pair=True
    )
    a_got = flip(a_give, "loop", 2)
    b_got = flip(b_give, "loop", 1)

    far_edge = after(far_edge, a_give)
    far_core_edge = flip(far_edge, "row", 1)
    far = flip(after(rest, far_edge, a_got, b_got), "row", 2)

    even, odd = pl.pallas_call(
        edge_kernel,
        grid=(1,),
        out_shape=(array((rows, half), F32),) * 2,
        in_specs=[
            pl.BlockSpec((rows, width), lambda i: (0, 0)),
            pl.BlockSpec((rows, width), lambda i: (0, 0)),
            pl.BlockSpec((rows, width), lambda i: (0, last)),
            pl.BlockSpec((rows, width), lambda i: (0, last)),
            pl.BlockSpec((2, piece, half), lambda i: (0, 0, 0)),
            pl.BlockSpec((1, piece, half), lambda i: (0, 0, 1)),
            pl.BlockSpec((1, piece, half), lambda i: (last, 0, 0)),
            pl.BlockSpec((2, piece, half), lambda i: (0, 0, 0)),
            pl.BlockSpec((2, piece, half), lambda i: (0, 0, 0)),
        ],
        out_specs=(pl.BlockSpec((rows, half), lambda i: (0, 0)),) * 2,
        scratch_shapes=[pltpu.VMEM((2, width, half), BF16)] * 2,
        compiler_params=params(20),
        cost_estimate=cost(0, 0),
    )(slab_hi, slab_lo, slab_hi, slab_lo, edge, core, core, far_edge, far_core_edge)
    quarters = (teams, piece, quarter)
    (held,) = glue(partial(meet_kernel, pairs), (quarters,), a_keep, b_keep, after(a_got, even), b_got, pair=True)
    even_in = trade(even, 0)
    odd_in = trade(after(odd, even_in), 1)

    bits = [1 << b for b in range(2, (loops - 1).bit_length())]
    got = flip(held, "loop", bits[0])
    for bit in bits[:-1]:
        (held,) = glue(partial(pick_kernel, pairs, bit), (quarters,), held, got, pair=True)
        got = flip(held, "loop", 2 * bit)
    far_core = flip(after(far, even_in, got), "row", 1)
    blocks = array((rows, columns), BF16)
    turned_hi, turned_lo = pl.pallas_call(
        turn_kernel,
        out_shape=(blocks, blocks),
        in_specs=[VMEM] * 9,
        out_specs=(VMEM, VMEM),
        scratch_shapes=[pltpu.VMEM((pairs, width, width), BF16)] * 2,
        compiler_params=params(28),
        cost_estimate=cost(0, 0),
    )(slab_hi, slab_lo, rest, core, far, far_core, even, odd, even_in)

    pieces = (2, piece, quarter)
    give, held = glue(partial(last_pick_kernel, pairs, bits[-1]), (pieces, pieces), held, got, pair=True)
    give, held = glue(cross_kernel, (pieces, pieces), held, after(flip(give, "row", 2), turned_hi, odd_in))
    more = flip(give, "row", 1)

    near = flip(held, "loop", 2), flip(more, "loop", 2)
    side = flip(held, "loop", 1), flip(more, "loop", 1)
    across = flip(near[0], "loop", 1), flip(side[1], "loop", 2)

    def left(offsets, pieces, out=None):
        tall = len(offsets) * quarter
        aliased = out is not None
        return pl.pallas_call(
            partial(left_kernel, offsets, int(aliased)),
            out_shape=array((rows, columns), F32),
            in_specs=[VMEM] * (len(pieces) + 3) + [HBM] * aliased,
            out_specs=HBM,
            input_output_aliases={len(pieces) + 3: 0} if aliased else {},
            scratch_shapes=[
                pltpu.VMEM((tall, columns), F32),
                pltpu.VMEM((width, tall), F32),
                pltpu.VMEM((tall, width), BF16),
                pltpu.VMEM((tall, width), BF16),
                pltpu.SemaphoreType.DMA((len(offsets), 2 * pairs)),
            ],
            compiler_params=params(20),
            cost_estimate=cost(0, 0),
        )(*pieces, turned_hi, turned_lo, odd_in, *([out] * aliased))

    out = left((0,), (held, more))
    out = left((1, 2), (*near, *side), out)
    return left((3,), across, out)


def solution(mesh):
    return jax.shard_map(
        per_device,
        mesh=mesh,
        in_specs=(P("row", "loop"), P("loop", "row", None), P()),
        out_specs=P("row", "loop"),
        check_vma=False,
    )
```

```python
from functools import partial

import jax
import jax.numpy as jnp
from jax import lax
from jax.experimental import pallas as pl
from jax.experimental.pallas import tpu as pltpu
from jax.sharding import PartitionSpec as P

VMEM = pl.BlockSpec(memory_space=pltpu.VMEM)
SMEM = pl.BlockSpec(memory_space=pltpu.SMEM)
HBM = pl.BlockSpec(memory_space=pltpu.HBM)
F32, BF16 = jnp.float32, jnp.bfloat16


def flip(x, axis, bit):
    n = lax.axis_size(axis)
    return lax.ppermute(x, axis, [(i, i ^ bit) for i in range(n)])


def trade(x, first):
    n = lax.axis_size("loop")
    pairs = []
    for i in range(first, n - 1, 2):
        pairs += [(i, i + 1), (i + 1, i)]
    return lax.ppermute(x, "loop", pairs)


def after(x, *others):
    return lax.optimization_barrier((x,) + others)[0]


def params(mib):
    return pltpu.CompilerParams(vmem_limit_bytes=mib << 20)


def cost(flops, bytes_accessed):
    return pl.CostEstimate(flops=flops, bytes_accessed=bytes_accessed, transcendentals=0)


def split(x):
    hi = x.astype(BF16)
    lo = (x - hi.astype(F32)).astype(BF16)
    return hi, lo


def dot3(a_hi, a_lo, b_hi, b_lo):
    def dot(a, b):
        return jnp.dot(a, b, preferred_element_type=F32)

    return dot(a_hi, b_hi) + (dot(a_hi, b_lo) + dot(a_lo, b_hi))


def copy_all(copies, sem):
    copies = [pltpu.make_async_copy(src, dst, sem.at[n]) for n, (src, dst) in enumerate(copies)]
    for copy in copies:
        copy.start()
    for copy in copies:
        copy.wait()


def candidate_kernel(home, pair_ref, rot_ref, a_ref, b_ref, sem):
    pairs, piece, width = rot_ref.shape
    chunk, half, quarter = piece // 2, width // 2, width // 4
    l = lax.axis_index("loop")
    side, up = l % 2, (l // 2) % 2
    if not home:
        side, up = 1 - side, 1 - up
    copies = []
    for t in range(a_ref.shape[0]):
        slot = pair_ref[t] % pairs
        copies.append((rot_ref.at[slot, :chunk, pl.ds(pl.multiple_of(side * half, half), half)], a_ref.at[t]))
        for s in range(2):
            cols = pl.ds(pl.multiple_of(s * half + up * quarter, quarter), quarter)
            copies.append((rot_ref.at[slot, chunk:, cols], b_ref.at[t, :, s * quarter : (s + 1) * quarter]))
    copy_all(copies, sem)


def cut_kernel(rot_ref, edge_ref, rest_ref, sem):
    pairs, _, width = rot_ref.shape
    half, last = width // 2, pairs - 1
    copies = [
        (rot_ref.at[0, :, half:], edge_ref.at[0]),
        (rot_ref.at[last, :, :half], edge_ref.at[1]),
        (rot_ref.at[0, :, :half], rest_ref.at[:, :half]),
        (rot_ref.at[last, :, half:], rest_ref.at[:, half + (last - 1) * width :]),
    ]
    for p in range(1, last):
        copies.append((rot_ref.at[p], rest_ref.at[:, half + (p - 1) * width : half + p * width]))
    copy_all(copies, sem)


def take(pair_ref, pairs, bit, t, kept, got):
    l = lax.axis_index("loop")
    return jnp.where(((pair_ref[t] // pairs) & bit) == (l & bit), kept, got)


def halve_kernel(pairs, pair_ref, a_kept, b_kept, a_got, b_got, a_give, b_give, a_keep, b_keep):
    l = lax.axis_index("loop")
    quarter = a_give.shape[-1]
    side, up = l % 2, (l // 2) % 2
    for bit, cut, kept, got, give, keep in (
        (1, up, a_kept, a_got, a_give, a_keep),
        (2, side, b_kept, b_got, b_give, b_keep),
    ):
        away = pl.ds(pl.multiple_of((1 - cut) * quarter, quarter), quarter)
        home = pl.ds(pl.multiple_of(cut * quarter, quarter), quarter)
        for t in range(give.shape[0]):
            give[t] = take(pair_ref, pairs, bit, t, kept[t, :, away], got[t, :, away])
            keep[t] = take(pair_ref, pairs, bit, t, kept[t, :, home], got[t, :, home])


def meet_kernel(pairs, pair_ref, a_kept, b_kept, a_got, b_got, out_ref):
    chunk = a_kept.shape[1]
    for t in range(out_ref.shape[0]):
        out_ref[t, :chunk] = take(pair_ref, pairs, 2, t, a_kept[t], a_got[t])
        out_ref[t, chunk:] = take(pair_ref, pairs, 1, t, b_kept[t], b_got[t])


def pick_kernel(pairs, bit, pair_ref, kept_ref, got_ref, out_ref):
    for t in range(out_ref.shape[0]):
        out_ref[t] = take(pair_ref, pairs, bit, t, kept_ref[t], got_ref[t])


def last_pick_kernel(pairs, bit, pair_ref, kept_ref, got_ref, give_ref, keep_ref):
    high = lax.axis_index("row") // 2
    for n in range(2):
        for ref, t in ((give_ref, 2 * (1 - high) + n), (keep_ref, 2 * high + n)):
            ref[n] = take(pair_ref, pairs, bit, t, kept_ref[t], got_ref[t])


def cross_kernel(kept_ref, got_ref, give_ref, keep_ref):
    odd = lax.axis_index("row") % 2
    for n, ref in enumerate((kept_ref, got_ref)):
        give_ref[n] = ref[1 - odd]
        keep_ref[n] = ref[odd]


def split_kernel(slab_ref, hi_ref, lo_ref):
    hi_ref[...], lo_ref[...] = split(slab_ref[...])


def stack_parts(hi_ref, lo_ref, n, parts):
    piece, wide = parts[0].shape
    r = lax.axis_index("row")
    for k, part in enumerate(parts):
        rows = pl.ds(pl.multiple_of((r ^ k) * piece, piece), piece)
        hi, lo = split(part)
        hi_ref[n, rows, :wide] = hi
        lo_ref[n, rows, :wide] = lo


def edge_kernel(shi0, slo0, shi1, slo1, own_ref, core0, core1, far_ref, far_core_ref, even_ref, odd_ref, hi_ref, lo_ref):
    side = lax.axis_index("loop") % 2
    for n, core in enumerate((core0, core1)):
        stack_parts(hi_ref, lo_ref, n, (own_ref[n], core[0], far_ref[n], far_core_ref[n]))
    bottom = dot3(shi0[...], slo0[...], hi_ref[0], lo_ref[0])
    top = dot3(shi1[...], slo1[...], hi_ref[1], lo_ref[1])

    @pl.when(side == 0)
    def _():
        even_ref[...] = top
        odd_ref[...] = bottom

    @pl.when(side == 1)
    def _():
        even_ref[...] = bottom
        odd_ref[...] = top


def turn_kernel(
    shi_ref, slo_ref, own_ref, core_ref, far_ref, far_core_ref, even_ref, odd_ref, even_in,
    thi_ref, tlo_ref, hi_ref, lo_ref,
):
    pairs, piece, width = core_ref.shape
    half, last = width // 2, pairs - 1
    l, loops = lax.axis_index("loop"), lax.axis_size("loop")
    for p in range(pairs):
        cols = slice(0, half) if p == 0 else slice(half, width) if p == last else slice(0, width)
        at = 0 if p == 0 else half + (p - 1) * width
        here = slice(at, at + cols.stop - cols.start)
        stack_parts(hi_ref, lo_ref, p, (own_ref[:, here], core_ref[p, :, cols], far_ref[:, here], far_core_ref[:, here]))

    def put(block, k):
        hi, lo = split(block)
        thi_ref[:, k * half : (k + 1) * half] = hi
        tlo_ref[:, k * half : (k + 1) * half] = lo

    for p in range(1, last):
        a_hi, a_lo = (ref[:, p * width : (p + 1) * width] for ref in (shi_ref, slo_ref))
        made = dot3(a_hi, a_lo, hi_ref[p], lo_ref[p])
        put(made[:, :half], 2 * (p + 1))
        put(made[:, half:], 2 * (p - 1) + 1)
    a_hi, a_lo = (ref[:, last * width :] for ref in (shi_ref, slo_ref))
    put(dot3(a_hi, a_lo, hi_ref[last, :, :half], lo_ref[last, :, :half]), 2 * (last - 1) + 1)
    a_hi, a_lo = (ref[:, :width] for ref in (shi_ref, slo_ref))
    top = dot3(a_hi, a_lo, hi_ref[0, :, :half], lo_ref[0, :, :half])
    put(jnp.where(l == 0, top, even_in[...]), 0)
    put(jnp.where(l == 0, odd_ref[...], top), 2)
    put(jnp.where(l == loops - 1, odd_ref[...], even_in[...]), 2 * pairs - 1)


def left_kernel(offsets, aliased, *refs):
    count = 2 * len(offsets)
    pieces, (thi_ref, tlo_ref, odd_ref) = refs[:count], refs[count : count + 3]
    out_ref, made_ref, rot_ref, hi_ref, lo_ref, sem = refs[count + 3 + aliased :]
    _, piece, quarter = pieces[0].shape
    width = thi_ref.shape[0]
    l, r = lax.axis_index("loop"), lax.axis_index("row")
    mine = 2 * (l % 2) + (l // 2) % 2
    for place, block in enumerate(pieces):
        n, core = divmod(place, 2)
        for m in range(2):
            rows = pl.ds(pl.multiple_of((r ^ (2 * m + core)) * piece, piece), piece)
            rot_ref[rows, n * quarter : (n + 1) * quarter] = block[m]
    hi_ref[...], lo_ref[...] = split(rot_ref[...].T)
    wide = width // 2
    blocks = made_ref.shape[1] // wide
    loops = lax.axis_size("loop")
    by_odd = {0: (l % 2 == 0) & (l > 0), blocks - 1: (l % 2 == 1) & (l < loops - 1)}
    copies = []
    for k in (*range(1, blocks - 1), 0, blocks - 1):
        cols = slice(k * wide, (k + 1) * wide)
        t_hi, t_lo = thi_ref[:, cols], tlo_ref[:, cols]
        if k in by_odd:
            came_hi, came_lo = split(odd_ref[...])
            t_hi, t_lo = jnp.where(by_odd[k], came_hi, t_hi), jnp.where(by_odd[k], came_lo, t_lo)
        made_ref[:, cols] = dot3(hi_ref[...], lo_ref[...], t_hi, t_lo)
        for n, offset in enumerate(offsets):
            rows = pl.ds(pl.multiple_of((mine ^ offset) * quarter, quarter), quarter)
            copy = pltpu.make_async_copy(
                made_ref.at[n * quarter : (n + 1) * quarter, cols], out_ref.at[rows, cols], sem.at[n, k]
            )
            copy.start()
            copies.append(copy)
    for copy in copies:
        copy.wait()


def per_device(slab, rotations, slab_pair):
    pairs, piece, width = rotations.shape
    half, quarter = width // 2, width // 4
    rows, columns = slab.shape
    loops, teams = lax.axis_size("loop"), lax.axis_size("row")
    last = pairs - 1
    array = jax.ShapeDtypeStruct

    def glue(kernel, shapes, *operands, pair=False):
        return pl.pallas_call(
            kernel,
            out_shape=tuple(array(shape, F32) for shape in shapes),
            in_specs=[SMEM] * pair + [VMEM] * len(operands),
            out_specs=(VMEM,) * len(shapes),
            compiler_params=params(4),
            cost_estimate=cost(0, 0),
        )(*([slab_pair] * pair), *operands)

    def copied(kernel, shapes, count, pair=False):
        return pl.pallas_call(
            kernel,
            out_shape=tuple(array(shape, F32) for shape in shapes),
            in_specs=[SMEM] * pair + [HBM],
            out_specs=(VMEM,) * len(shapes),
            scratch_shapes=[pltpu.SemaphoreType.DMA((count,))],
            compiler_params=params(4),
            cost_estimate=cost(0, 0),
        )

    transforms = pltpu.with_memory_space_constraint(rotations, pltpu.HBM)
    chunks = (teams, piece // 2, half)
    a_give, b_give = copied(partial(candidate_kernel, False), (chunks, chunks), 3 * teams, pair=True)(
        slab_pair, transforms
    )
    edge, rest = copied(cut_kernel, ((2, piece, half), (piece, last * width)), pairs + 2)(after(transforms, a_give))
    a_keep, b_keep = copied(partial(candidate_kernel, True), (chunks, chunks), 3 * teams, pair=True)(
        slab_pair, after(transforms, edge)
    )

    a_got = flip(a_give, "loop", 1)
    b_got = flip(b_give, "loop", 2)
    far_edge = flip(edge, "row", 2)
    core = flip(rotations, "row", 1)

    slab_hi, slab_lo = pl.pallas_call(
        split_kernel,
        grid=(4,),
        out_shape=(array((rows, columns), BF16),) * 2,
        in_specs=[pl.BlockSpec((rows // 4, columns), lambda i: (i, 0))],
        out_specs=(pl.BlockSpec((rows // 4, columns), lambda i: (i, 0)),) * 2,
        compiler_params=params(8),
        cost_estimate=cost(0, 0),
    )(pltpu.with_memory_space_constraint(after(slab, a_keep), pltpu.HBM))

    fine = (teams, piece // 2, quarter)
    a_give, b_give, a_keep, b_keep = glue(
        partial(halve_kernel, pairs), (fine,) * 4, a_keep, b_keep, after(a_got, slab_hi), b_got, pair=True
    )
    a_got = flip(a_give, "loop", 2)
    b_got = flip(b_give, "loop", 1)

    far_edge = after(far_edge, a_give)
    far_core_edge = flip(far_edge, "row", 1)
    far = flip(after(rest, far_edge, a_got, b_got), "row", 2)

    even, odd = pl.pallas_call(
        edge_kernel,
        grid=(1,),
        out_shape=(array((rows, half), F32),) * 2,
        in_specs=[
            pl.BlockSpec((rows, width), lambda i: (0, 0)),
            pl.BlockSpec((rows, width), lambda i: (0, 0)),
            pl.BlockSpec((rows, width), lambda i: (0, last)),
            pl.BlockSpec((rows, width), lambda i: (0, last)),
            pl.BlockSpec((2, piece, half), lambda i: (0, 0, 0)),
            pl.BlockSpec((1, piece, half), lambda i: (0, 0, 1)),
            pl.BlockSpec((1, piece, half), lambda i: (last, 0, 0)),
            pl.BlockSpec((2, piece, half), lambda i: (0, 0, 0)),
            pl.BlockSpec((2, piece, half), lambda i: (0, 0, 0)),
        ],
        out_specs=(pl.BlockSpec((rows, half), lambda i: (0, 0)),) * 2,
        scratch_shapes=[pltpu.VMEM((2, width, half), BF16)] * 2,
        compiler_params=params(20),
        cost_estimate=cost(0, 0),
    )(slab_hi, slab_lo, slab_hi, slab_lo, edge, core, core, far_edge, far_core_edge)
    quarters = (teams, piece, quarter)
    (held,) = glue(partial(meet_kernel, pairs), (quarters,), a_keep, b_keep, after(a_got, even), b_got, pair=True)
    even_in = trade(even, 0)
    odd_in = trade(after(odd, even_in), 1)

    bits = [1 << b for b in range(2, (loops - 1).bit_length())]
    got = flip(held, "loop", bits[0])
    for bit in bits[:-1]:
        (held,) = glue(partial(pick_kernel, pairs, bit), (quarters,), held, got, pair=True)
        got = flip(held, "loop", 2 * bit)
    far_core = flip(after(far, even_in, got), "row", 1)
    blocks = array((rows, columns), BF16)
    turned_hi, turned_lo = pl.pallas_call(
        turn_kernel,
        out_shape=(blocks, blocks),
        in_specs=[VMEM] * 9,
        out_specs=(VMEM, VMEM),
        scratch_shapes=[pltpu.VMEM((pairs, width, width), BF16)] * 2,
        compiler_params=params(28),
        cost_estimate=cost(0, 0),
    )(slab_hi, slab_lo, rest, core, far, far_core, even, odd, even_in)

    pieces = (2, piece, quarter)
    give, held = glue(partial(last_pick_kernel, pairs, bits[-1]), (pieces, pieces), held, got, pair=True)
    give, held = glue(cross_kernel, (pieces, pieces), held, after(flip(give, "row", 2), turned_hi))
    more = flip(give, "row", 1)

    near = after(flip(held, "loop", 2), odd_in), flip(more, "loop", 2)
    side = flip(held, "loop", 1), flip(more, "loop", 1)
    across = flip(near[0], "loop", 1), flip(side[1], "loop", 2)

    def left(offsets, pieces, out=None):
        tall = len(offsets) * quarter
        aliased = out is not None
        return pl.pallas_call(
            partial(left_kernel, offsets, int(aliased)),
            out_shape=array((rows, columns), F32),
            in_specs=[VMEM] * (len(pieces) + 3) + [HBM] * aliased,
            out_specs=HBM,
            input_output_aliases={len(pieces) + 3: 0} if aliased else {},
            scratch_shapes=[
                pltpu.VMEM((tall, columns), F32),
                pltpu.VMEM((width, tall), F32),
                pltpu.VMEM((tall, width), BF16),
                pltpu.VMEM((tall, width), BF16),
                pltpu.SemaphoreType.DMA((len(offsets), 2 * pairs)),
            ],
            compiler_params=params(20),
            cost_estimate=cost(0, 0),
        )(*pieces, turned_hi, turned_lo, odd_in, *([out] * aliased))

    out = left((0,), (held, more))
    out = left((1, 2), (*near, *side), out)
    return left((3,), across, out)


def solution(mesh):
    return jax.shard_map(
        per_device,
        mesh=mesh,
        in_specs=(P("row", "loop"), P("loop", "row", None), P()),
        out_specs=P("row", "loop"),
        check_vma=False,
    )
```

```python
from functools import partial

import jax
import jax.numpy as jnp
from jax import lax
from jax.experimental import pallas as pl
from jax.experimental.pallas import tpu as pltpu
from jax.sharding import PartitionSpec as P

VMEM = pl.BlockSpec(memory_space=pltpu.VMEM)
SMEM = pl.BlockSpec(memory_space=pltpu.SMEM)
HBM = pl.BlockSpec(memory_space=pltpu.HBM)
F32, BF16 = jnp.float32, jnp.bfloat16


def flip(x, axis, bit):
    n = lax.axis_size(axis)
    return lax.ppermute(x, axis, [(i, i ^ bit) for i in range(n)])


def trade(x, first):
    n = lax.axis_size("loop")
    pairs = []
    for i in range(first, n - 1, 2):
        pairs += [(i, i + 1), (i + 1, i)]
    return lax.ppermute(x, "loop", pairs)


def after(x, *others):
    return lax.optimization_barrier((x,) + others)[0]


def params(mib):
    return pltpu.CompilerParams(vmem_limit_bytes=mib << 20)


def cost(flops, bytes_accessed):
    return pl.CostEstimate(flops=flops, bytes_accessed=bytes_accessed, transcendentals=0)


def split(x):
    hi = x.astype(BF16)
    lo = (x - hi.astype(F32)).astype(BF16)
    return hi, lo


def dot3(a_hi, a_lo, b_hi, b_lo):
    def dot(a, b):
        return jnp.dot(a, b, preferred_element_type=F32)

    return dot(a_hi, b_hi) + (dot(a_hi, b_lo) + dot(a_lo, b_hi))


def copy_all(copies, sem):
    copies = [pltpu.make_async_copy(src, dst, sem.at[n]) for n, (src, dst) in enumerate(copies)]
    for copy in copies:
        copy.start()
    for copy in copies:
        copy.wait()


def candidate_kernel(home, pair_ref, rot_ref, a_ref, b_ref, sem):
    pairs, piece, width = rot_ref.shape
    chunk, half, quarter = piece // 2, width // 2, width // 4
    l = lax.axis_index("loop")
    side, up = l % 2, (l // 2) % 2
    if not home:
        side, up = 1 - side, 1 - up
    copies = []
    for t in range(a_ref.shape[0]):
        slot = pair_ref[t] % pairs
        copies.append((rot_ref.at[slot, :chunk, pl.ds(pl.multiple_of(side * half, half), half)], a_ref.at[t]))
        for s in range(2):
            cols = pl.ds(pl.multiple_of(s * half + up * quarter, quarter), quarter)
            copies.append((rot_ref.at[slot, chunk:, cols], b_ref.at[t, :, s * quarter : (s + 1) * quarter]))
    copy_all(copies, sem)


def cut_kernel(rot_ref, edge_ref, rest_ref, sem):
    pairs, _, width = rot_ref.shape
    half, last = width // 2, pairs - 1
    copies = [
        (rot_ref.at[0, :, half:], edge_ref.at[0]),
        (rot_ref.at[last, :, :half], edge_ref.at[1]),
        (rot_ref.at[0, :, :half], rest_ref.at[:, :half]),
        (rot_ref.at[last, :, half:], rest_ref.at[:, half + (last - 1) * width :]),
    ]
    for p in range(1, last):
        copies.append((rot_ref.at[p], rest_ref.at[:, half + (p - 1) * width : half + p * width]))
    copy_all(copies, sem)


def take(pair_ref, pairs, bit, t, kept, got):
    l = lax.axis_index("loop")
    return jnp.where(((pair_ref[t] // pairs) & bit) == (l & bit), kept, got)


def halve_kernel(pairs, pair_ref, a_kept, b_kept, a_got, b_got, a_give, b_give, a_keep, b_keep):
    l = lax.axis_index("loop")
    quarter = a_give.shape[-1]
    side, up = l % 2, (l // 2) % 2
    for bit, cut, kept, got, give, keep in (
        (1, up, a_kept, a_got, a_give, a_keep),
        (2, side, b_kept, b_got, b_give, b_keep),
    ):
        away = pl.ds(pl.multiple_of((1 - cut) * quarter, quarter), quarter)
        home = pl.ds(pl.multiple_of(cut * quarter, quarter), quarter)
        for t in range(give.shape[0]):
            give[t] = take(pair_ref, pairs, bit, t, kept[t, :, away], got[t, :, away])
            keep[t] = take(pair_ref, pairs, bit, t, kept[t, :, home], got[t, :, home])


def meet_kernel(pairs, pair_ref, a_kept, b_kept, a_got, b_got, out_ref):
    chunk = a_kept.shape[1]
    for t in range(out_ref.shape[0]):
        out_ref[t, :chunk] = take(pair_ref, pairs, 2, t, a_kept[t], a_got[t])
        out_ref[t, chunk:] = take(pair_ref, pairs, 1, t, b_kept[t], b_got[t])


def pick_kernel(pairs, bit, pair_ref, kept_ref, got_ref, out_ref):
    for t in range(out_ref.shape[0]):
        out_ref[t] = take(pair_ref, pairs, bit, t, kept_ref[t], got_ref[t])


def last_pick_kernel(pairs, bit, pair_ref, kept_ref, got_ref, give_ref, keep_ref):
    high = lax.axis_index("row") // 2
    for n in range(2):
        for ref, t in ((give_ref, 2 * (1 - high) + n), (keep_ref, 2 * high + n)):
            ref[n] = take(pair_ref, pairs, bit, t, kept_ref[t], got_ref[t])


def cross_kernel(kept_ref, got_ref, give_ref, keep_ref):
    odd = lax.axis_index("row") % 2
    for n, ref in enumerate((kept_ref, got_ref)):
        give_ref[n] = ref[1 - odd]
        keep_ref[n] = ref[odd]


def split_kernel(slab_ref, hi_ref, lo_ref):
    hi_ref[...], lo_ref[...] = split(slab_ref[...])


def stack_parts(hi_ref, lo_ref, n, parts):
    piece, wide = parts[0].shape
    r = lax.axis_index("row")
    for k, part in enumerate(parts):
        rows = pl.ds(pl.multiple_of((r ^ k) * piece, piece), piece)
        hi, lo = split(part)
        hi_ref[n, rows, :wide] = hi
        lo_ref[n, rows, :wide] = lo


def edge_kernel(shi0, slo0, shi1, slo1, own_ref, core0, core1, far_ref, far_core_ref, even_ref, odd_ref, hi_ref, lo_ref):
    side = lax.axis_index("loop") % 2
    for n, core in enumerate((core0, core1)):
        stack_parts(hi_ref, lo_ref, n, (own_ref[n], core[0], far_ref[n], far_core_ref[n]))
    bottom = dot3(shi0[...], slo0[...], hi_ref[0], lo_ref[0])
    top = dot3(shi1[...], slo1[...], hi_ref[1], lo_ref[1])

    @pl.when(side == 0)
    def _():
        even_ref[...] = top
        odd_ref[...] = bottom

    @pl.when(side == 1)
    def _():
        even_ref[...] = bottom
        odd_ref[...] = top


def turn_kernel(
    shi_ref, slo_ref, own_ref, core_ref, far_ref, far_core_ref, even_ref, odd_ref, even_in,
    thi_ref, tlo_ref, hi_ref, lo_ref,
):
    pairs, piece, width = core_ref.shape
    half, last = width // 2, pairs - 1
    l, loops = lax.axis_index("loop"), lax.axis_size("loop")
    for p in range(pairs):
        cols = slice(0, half) if p == 0 else slice(half, width) if p == last else slice(0, width)
        at = 0 if p == 0 else half + (p - 1) * width
        here = slice(at, at + cols.stop - cols.start)
        stack_parts(hi_ref, lo_ref, p, (own_ref[:, here], core_ref[p, :, cols], far_ref[:, here], far_core_ref[:, here]))

    def put(block, k):
        hi, lo = split(block)
        thi_ref[:, k * half : (k + 1) * half] = hi
        tlo_ref[:, k * half : (k + 1) * half] = lo

    for p in range(1, last):
        a_hi, a_lo = (ref[:, p * width : (p + 1) * width] for ref in (shi_ref, slo_ref))
        made = dot3(a_hi, a_lo, hi_ref[p], lo_ref[p])
        put(made[:, :half], 2 * (p + 1))
        put(made[:, half:], 2 * (p - 1) + 1)
    a_hi, a_lo = (ref[:, last * width :] for ref in (shi_ref, slo_ref))
    put(dot3(a_hi, a_lo, hi_ref[last, :, :half], lo_ref[last, :, :half]), 2 * (last - 1) + 1)
    a_hi, a_lo = (ref[:, :width] for ref in (shi_ref, slo_ref))
    top = dot3(a_hi, a_lo, hi_ref[0, :, :half], lo_ref[0, :, :half])
    put(jnp.where(l == 0, top, even_in[...]), 0)
    put(jnp.where(l == 0, odd_ref[...], top), 2)
    put(jnp.where(l == loops - 1, odd_ref[...], even_in[...]), 2 * pairs - 1)


def left_kernel(offsets, aliased, *refs):
    count = 2 * len(offsets)
    pieces, (thi_ref, tlo_ref, odd_ref) = refs[:count], refs[count : count + 3]
    out_ref, made_ref, rot_ref, hi_ref, lo_ref, sem = refs[count + 3 + aliased :]
    _, piece, quarter = pieces[0].shape
    width = thi_ref.shape[0]
    l, r = lax.axis_index("loop"), lax.axis_index("row")
    mine = 2 * (l % 2) + (l // 2) % 2
    for place, block in enumerate(pieces):
        n, core = divmod(place, 2)
        for m in range(2):
            rows = pl.ds(pl.multiple_of((r ^ (2 * m + core)) * piece, piece), piece)
            rot_ref[rows, n * quarter : (n + 1) * quarter] = block[m]
    hi_ref[...], lo_ref[...] = split(rot_ref[...].T)
    wide = width // 2
    blocks = made_ref.shape[1] // wide
    loops = lax.axis_size("loop")
    by_odd = {0: (l % 2 == 0) & (l > 0), blocks - 1: (l % 2 == 1) & (l < loops - 1)}
    copies = []
    for k in (*range(1, blocks - 1), 0, blocks - 1):
        cols = slice(k * wide, (k + 1) * wide)
        t_hi, t_lo = thi_ref[:, cols], tlo_ref[:, cols]
        if k in by_odd:
            came_hi, came_lo = split(odd_ref[...])
            t_hi, t_lo = jnp.where(by_odd[k], came_hi, t_hi), jnp.where(by_odd[k], came_lo, t_lo)
        made_ref[:, cols] = dot3(hi_ref[...], lo_ref[...], t_hi, t_lo)
        for n, offset in enumerate(offsets):
            rows = pl.ds(pl.multiple_of((mine ^ offset) * quarter, quarter), quarter)
            copy = pltpu.make_async_copy(
                made_ref.at[n * quarter : (n + 1) * quarter, cols], out_ref.at[rows, cols], sem.at[n, k]
            )
            copy.start()
            copies.append(copy)
    for copy in copies:
        copy.wait()


def per_device(slab, rotations, slab_pair):
    pairs, piece, width = rotations.shape
    half, quarter = width // 2, width // 4
    rows, columns = slab.shape
    loops, teams = lax.axis_size("loop"), lax.axis_size("row")
    last = pairs - 1
    array = jax.ShapeDtypeStruct

    def glue(kernel, shapes, *operands, pair=False):
        return pl.pallas_call(
            kernel,
            out_shape=tuple(array(shape, F32) for shape in shapes),
            in_specs=[SMEM] * pair + [VMEM] * len(operands),
            out_specs=(VMEM,) * len(shapes),
            compiler_params=params(4),
            cost_estimate=cost(0, 0),
        )(*([slab_pair] * pair), *operands)

    def copied(kernel, shapes, count, pair=False):
        return pl.pallas_call(
            kernel,
            out_shape=tuple(array(shape, F32) for shape in shapes),
            in_specs=[SMEM] * pair + [HBM],
            out_specs=(VMEM,) * len(shapes),
            scratch_shapes=[pltpu.SemaphoreType.DMA((count,))],
            compiler_params=params(4),
            cost_estimate=cost(0, 0),
        )

    transforms = pltpu.with_memory_space_constraint(rotations, pltpu.HBM)
    chunks = (teams, piece // 2, half)
    a_give, b_give = copied(partial(candidate_kernel, False), (chunks, chunks), 3 * teams, pair=True)(
        slab_pair, transforms
    )
    edge, rest = copied(cut_kernel, ((2, piece, half), (piece, last * width)), pairs + 2)(after(transforms, a_give))
    a_keep, b_keep = copied(partial(candidate_kernel, True), (chunks, chunks), 3 * teams, pair=True)(
        slab_pair, after(transforms, edge)
    )

    a_got = flip(a_give, "loop", 1)
    b_got = flip(b_give, "loop", 2)
    far_edge = flip(edge, "row", 2)
    core = flip(rotations, "row", 1)

    slab_hi, slab_lo = pl.pallas_call(
        split_kernel,
        grid=(4,),
        out_shape=(array((rows, columns), BF16),) * 2,
        in_specs=[pl.BlockSpec((rows // 4, columns), lambda i: (i, 0))],
        out_specs=(pl.BlockSpec((rows // 4, columns), lambda i: (i, 0)),) * 2,
        compiler_params=params(8),
        cost_estimate=cost(0, 0),
    )(pltpu.with_memory_space_constraint(after(slab, a_keep), pltpu.HBM))

    fine = (teams, piece // 2, quarter)
    a_give, b_give, a_keep, b_keep = glue(
        partial(halve_kernel, pairs), (fine,) * 4, a_keep, b_keep, after(a_got, slab_hi), b_got, pair=True
    )
    a_got = flip(a_give, "loop", 2)
    b_got = flip(b_give, "loop", 1)

    far_edge = after(far_edge, a_give)
    far_core_edge = flip(far_edge, "row", 1)
    far = flip(after(rest, far_edge, a_got, b_got), "row", 2)

    even, odd = pl.pallas_call(
        edge_kernel,
        grid=(1,),
        out_shape=(array((rows, half), F32),) * 2,
        in_specs=[
            pl.BlockSpec((rows, width), lambda i: (0, 0)),
            pl.BlockSpec((rows, width), lambda i: (0, 0)),
            pl.BlockSpec((rows, width), lambda i: (0, last)),
            pl.BlockSpec((rows, width), lambda i: (0, last)),
            pl.BlockSpec((2, piece, half), lambda i: (0, 0, 0)),
            pl.BlockSpec((1, piece, half), lambda i: (0, 0, 1)),
            pl.BlockSpec((1, piece, half), lambda i: (last, 0, 0)),
            pl.BlockSpec((2, piece, half), lambda i: (0, 0, 0)),
            pl.BlockSpec((2, piece, half), lambda i: (0, 0, 0)),
        ],
        out_specs=(pl.BlockSpec((rows, half), lambda i: (0, 0)),) * 2,
        scratch_shapes=[pltpu.VMEM((2, width, half), BF16)] * 2,
        compiler_params=params(20),
        cost_estimate=cost(0, 0),
    )(slab_hi, slab_lo, slab_hi, slab_lo, edge, core, core, far_edge, far_core_edge)
    quarters = (teams, piece, quarter)
    (held,) = glue(partial(meet_kernel, pairs), (quarters,), a_keep, b_keep, after(a_got, even), b_got, pair=True)
    even_in = trade(even, 0)
    odd_in = trade(after(odd, even_in), 1)

    bits = [1 << b for b in range(2, (loops - 1).bit_length())]
    got = flip(held, "loop", bits[0])
    for bit in bits[:-1]:
        (held,) = glue(partial(pick_kernel, pairs, bit), (quarters,), held, got, pair=True)
        got = flip(held, "loop", 2 * bit)
    far_core = flip(after(far, even_in, got), "row", 1)
    blocks = array((rows, columns), BF16)
    turned_hi, turned_lo = pl.pallas_call(
        turn_kernel,
        out_shape=(blocks, blocks),
        in_specs=[VMEM] * 9,
        out_specs=(VMEM, VMEM),
        scratch_shapes=[pltpu.VMEM((pairs, width, width), BF16)] * 2,
        compiler_params=params(28),
        cost_estimate=cost(0, 0),
    )(slab_hi, slab_lo, rest, core, far, far_core, even, odd, even_in)

    pieces = (2, piece, quarter)
    give, held = glue(partial(last_pick_kernel, pairs, bits[-1]), (pieces, pieces), held, got, pair=True)
    give, held = glue(cross_kernel, (pieces, pieces), held, after(flip(give, "row", 2), turned_hi))
    more = flip(give, "row", 1)

    near = flip(held, "loop", 2), after(flip(more, "loop", 2), odd_in)
    side = flip(held, "loop", 1), flip(more, "loop", 1)
    across = flip(near[0], "loop", 1), flip(side[1], "loop", 2)

    def left(offsets, pieces, out=None):
        tall = len(offsets) * quarter
        aliased = out is not None
        return pl.pallas_call(
            partial(left_kernel, offsets, int(aliased)),
            out_shape=array((rows, columns), F32),
            in_specs=[VMEM] * (len(pieces) + 3) + [HBM] * aliased,
            out_specs=HBM,
            input_output_aliases={len(pieces) + 3: 0} if aliased else {},
            scratch_shapes=[
                pltpu.VMEM((tall, columns), F32),
                pltpu.VMEM((width, tall), F32),
                pltpu.VMEM((tall, width), BF16),
                pltpu.VMEM((tall, width), BF16),
                pltpu.SemaphoreType.DMA((len(offsets), 2 * pairs)),
            ],
            compiler_params=params(20),
            cost_estimate=cost(0, 0),
        )(*pieces, turned_hi, turned_lo, odd_in, *([out] * aliased))

    out = left((0,), (held, more))
    out = left((1, 2), (*near, *side), out)
    return left((3,), across, out)


def solution(mesh):
    return jax.shard_map(
        per_device,
        mesh=mesh,
        in_specs=(P("row", "loop"), P("loop", "row", None), P()),
        out_specs=P("row", "loop"),
        check_vma=False,
    )
```
